32 devices in a mesh: groups: 2 (over y), ctx: 4 (over z), head: 4 (over x, core).
Axes of the slice: x: 2, y: 2, z: 4, core: 2. Of those that a mesh axis runs over, the one named last changes fastest.
Arguments:
- queries: bfloat16 [65536, 2048], P(('groups', 'ctx'), 'head'), parts along dimension 0, may hold values from -9 to 9
- keys: bfloat16 [65536, 1024], P(('groups', 'ctx'), 'head'), parts along dimension 0, may hold values from -6 to 6
- values: bfloat16 [65536, 1024], P(('groups', 'ctx'), 'head'), parts along dimension 0, may hold values from -6 to 6
- doc_lengths: int32 [32], P('groups'), parts along dimension 0, may hold values from 1 to 8192, 32768 in all
- live_blocks: int32 [8], P('groups'), parts along dimension 0, may hold values from 1 to 16, as said below
Outputs:
- attended: bfloat16 [65536, 2048], P(('groups', 'ctx'), 'head'), parts along dimension 0
- log_norm: float32 [32, 32768], P(('groups', 'head'), 'ctx'), parts along dimension 0
The draws below stay inside these ranges and needn't reach their ends.
There are 2 independent parts, one for each index of `groups`. The reference program is written for one: setup_inputs(seed, part) draws one part's arguments, and reference() takes and returns one part's arrays. A program takes and returns all parts, laid end to end along the dimension named above; each array names one. Nothing has to cross between parts.
Inputs may be any that keep to these rules, and one draw needn't show every extreme that they name: `live_blocks`: shards are paired heavy with light: for every shard s below 2, one of shards s and s + 2 has 16 scored blocks and the other fewer than 16.
All inputs are finite; a program needn't handle non-finite values.
Results may differ from the reference program's by a relative error of at most 0.0043.
Values may be sent and summed in bfloat16 or wider, within the bound.
A program may use at most 128 MiB of HBM per device.

```python
import math
import jax
import jax.numpy as jnp
import numpy as np
from jax import lax

HD = 128
QH = 16
KVH = 8
W = 1024
BLK = 512
DOCS = 16
SEQ_DEV = 8192
SEQ = 32768
NBLK = 16
SHARDS = 4


def query_key_pair(key):
    base = jax.random.fold_in(key, 11)
    key_query, key_keys = jax.random.split(base, 2)
    query_vals = jnp.clip(jax.random.normal(key_query, (SEQ, QH * HD), jnp.float32), -6.0, 6.0)
    key_vals = jnp.clip(jax.random.normal(key_keys, (SEQ, KVH * HD), jnp.float32), -6.0, 6.0)
    return (query_vals, key_vals)


def draw_queries(key, part):
    query_vals, key_vals = query_key_pair(key)
    return query_vals.astype(jnp.bfloat16)


def draw_keys(key, part):
    query_vals, key_vals = query_key_pair(key)
    return key_vals.astype(jnp.bfloat16)


def draw_live_blocks(key, part):
    key_side = jax.random.fold_in(key, 5)
    key_light = jax.random.fold_in(key, 6)
    half_shards = SHARDS // 2
    low_heavy = jax.random.randint(key_side, (half_shards,), 0, 2) == 0
    light_counts = jax.random.randint(key_light, (half_shards,), 1, NBLK)
    low_counts = jnp.where(low_heavy, NBLK, light_counts)
    high_counts = jnp.where(low_heavy, light_counts, NBLK)
    return jnp.concatenate([low_counts, high_counts]).astype(jnp.int32)


def level_of(stream_key, shape, cuts, smallest, top_value):
    level = 1.0
    for position, shards_of in cuts:
        heights = jax.random.uniform(jax.random.fold_in(jax.random.fold_in(stream_key, 6), position), (shards_of,), jnp.float32, smallest / len(cuts), top_value / len(cuts))
        level = level * jnp.repeat(jnp.exp(heights), shape[position] // shards_of).reshape((-1,) + (1,) * (len(shape) - 1 - position))
    return level


def length_profile(count, total, bound, skew):
    portions = [(1 << 20) // math.isqrt(standing ** skew) + 1 for standing in range(2, count + 1)]
    spare, given = total - bound - (count - 1), [1] * (count - 1)
    while spare > 0:
        candidates = [i for i in range(count - 1) if given[i] < bound]
        mass, left = sum([portions[i] for i in candidates]), spare
        for i in candidates:
            extra = min(bound - given[i], max(1, left * portions[i] // mass), spare)
            given[i] = given[i] + extra
            spare = spare - extra
    return np.array([bound] + given)


def uneven(key, count, total, reach, slope):
    if count == 2:
        one = jax.random.randint(key, (), max(1, total - reach), min(reach, total - 1) + 1)
        return jnp.stack([one, total - one])
    sizes = jnp.asarray(length_profile(count, total, reach, slope), jnp.int32)
    couples = (count - 1) // 2
    giver, receiver = sizes[1:1 + 2 * couples:2], sizes[2:2 + 2 * couples:2]
    margin = jnp.minimum(giver - 1, reach - receiver)
    moved = jax.random.randint(jax.random.fold_in(key, 1), (couples,), 0, 1 << 20) % (margin + 1)
    sizes = sizes.at[1:1 + 2 * couples:2].set(giver - moved).at[2:2 + 2 * couples:2].set(receiver + moved)
    return sizes[jax.random.permutation(jax.random.fold_in(key, 2), count)]


def bell_draw(key, dims, scale, bound, shards=(), held_as=jnp.bfloat16):
    gain = level_of(key, dims, shards, -0.22, 0.18) if shards else 1.0
    values = jax.random.normal(key, dims, jnp.float32) * scale * gain
    return jnp.minimum(jnp.maximum(values, -bound), bound).astype(held_as)


def setup_inputs(seed: int = 0, part: int = 0) -> dict:
    arg_keys = jax.random.split(jax.random.key(seed), 6)
    part_keys = jax.random.split(jax.random.fold_in(arg_keys[5], part), 6)
    queries = draw_queries(jax.random.fold_in(jax.random.fold_in(arg_keys[5], part), 71), part)
    keys = draw_keys(jax.random.fold_in(jax.random.fold_in(arg_keys[5], part), 71), part)
    values = bell_draw(part_keys[2], (SEQ, KVH * HD), 1.0, 6.0, ((0, 4), (1, 4)))
    doc_lengths = uneven(part_keys[3], DOCS, SEQ, SEQ // 4, 2).astype(jnp.int32)
    live_blocks = draw_live_blocks(jax.random.fold_in(jax.random.fold_in(arg_keys[5], part), 71), part)
    return {"queries": queries, "keys": keys, "values": values, "doc_lengths": doc_lengths, "live_blocks": live_blocks}


score_scale = 168.0 ** -0.5


def doc_index(starts, positions):
    return jnp.sum((starts[None, :] <= positions[:, None]).astype(jnp.int32), axis=1) - 1


def reference(queries, keys, values, doc_lengths, live_blocks):
    starts = (jnp.cumsum(doc_lengths) - doc_lengths).astype(jnp.int32)
    zero_rows = jnp.zeros((W, KVH * HD), keys.dtype)
    keys_pad = jnp.concatenate([zero_rows, keys], axis=0)
    values_pad = jnp.concatenate([zero_rows, values], axis=0)
    span = W + BLK

    def one_block(block_idx):
        row_start = (block_idx * BLK).astype(jnp.int32)
        shard_id = row_start // SEQ_DEV
        local_block = (row_start % SEQ_DEV) // BLK
        alive = local_block < live_blocks[shard_id]

        def compute(unused):
            query_blk = lax.dynamic_slice_in_dim(queries, row_start, BLK, 0).astype(jnp.float32).reshape(BLK, KVH, 2, HD)
            key_blk = lax.dynamic_slice_in_dim(keys_pad, row_start, span, 0).astype(jnp.float32).reshape(span, KVH, HD)
            value_blk = lax.dynamic_slice_in_dim(values_pad, row_start, span, 0).astype(jnp.float32).reshape(span, KVH, HD)
            scores = jnp.einsum("qhgd,khd->hgqk", query_blk, key_blk) * score_scale
            query_pos = row_start + jnp.arange(BLK, dtype=jnp.int32)
            key_pos = row_start - W + jnp.arange(span, dtype=jnp.int32)
            allowed = (doc_index(starts, key_pos)[None, :] == doc_index(starts, query_pos)[:, None])
            allowed = allowed & (key_pos[None, :] <= query_pos[:, None]) & (key_pos[None, :] > query_pos[:, None] - W) & (key_pos[None, :] >= 0)
            allowed = allowed[None, None]
            top = jnp.max(jnp.where(allowed, scores, -jnp.inf), axis=-1, keepdims=True)
            probs = jnp.where(allowed, jnp.exp(scores - top), 0.0)
            total = jnp.sum(probs, axis=-1)
            weights = lax.optimization_barrier(probs.astype(jnp.bfloat16)).astype(jnp.float32)
            mixed = jnp.einsum("hgqk,khd->qhgd", weights, value_blk) / jnp.transpose(total, (2, 0, 1))[..., None]
            attended = mixed.astype(jnp.bfloat16).reshape(BLK, QH * HD)
            log_norm = (top[..., 0] + jnp.log(total)).reshape(QH, BLK)
            return attended, log_norm

        def empty(unused):
            return jnp.zeros((BLK, QH * HD), jnp.bfloat16), jnp.zeros((QH, BLK), jnp.float32)

        return lax.cond(alive, compute, empty, 0)

    attended, log_norm = lax.map(one_block, jnp.arange(SEQ // BLK, dtype=jnp.int32))
    return attended.reshape(SEQ, QH * HD), jnp.transpose(log_norm, (1, 0, 2)).reshape(QH, SEQ)
```

```python
import functools
import math

import jax
import jax.numpy as jnp
from jax import lax
from jax.experimental import pallas as pl
from jax.experimental.pallas import tpu as pltpu
from jax.sharding import PartitionSpec as P

HD = 128
W = 1024
BLK = 512
TILE = 256
SPAN = W // TILE + 1

score_scale = 168.0 ** (-0.5)
log2_scale = score_scale * math.log2(math.e)
MASKED = -1e30


def from_behind(shard, axis, by):
    devices = lax.axis_size(axis)
    pairs = [(i, i + by) for i in range(devices) if 0 <= i + by < devices]
    return lax.ppermute(shard, axis, pairs)


def kernel(first, aliased, info, lengths, q_ref, k_ref, v_ref, pk_ref, pv_ref, *rest):
    out_ref, norm_ref, kbuf, vbuf = rest[2:] if aliased else rest
    step = pl.program_id(0)
    tile = step + first
    live = tile < info[1] * (BLK // TILE)
    kv_heads = k_ref.shape[1] // HD
    docs = lengths.shape[0]

    @pl.when(step == 0)
    def _():
        kbuf[:W, :] = pk_ref[...]
        vbuf[:, :W] = pv_ref[...].T

    @pl.when(jnp.logical_not(live))
    def _():
        out_ref[...] = jnp.zeros_like(out_ref)
        norm_ref[...] = jnp.zeros_like(norm_ref)

    @pl.when(live)
    def _():
        off = pl.multiple_of(step * TILE, TILE)
        kbuf[pl.ds(pl.multiple_of(off + W, TILE), TILE), :] = k_ref[...]
        vbuf[:, pl.ds(pl.multiple_of(off + W, TILE), TILE)] = v_ref[...].T

        t0 = info[0] + tile * TILE
        lane = lax.broadcasted_iota(jnp.int32, (1, TILE), 1)
        pos = t0 + lane
        doc_row = jnp.zeros((1, TILE), jnp.int32)
        doc_first = jnp.int32(0)
        doc_last = jnp.int32(0)
        start = jnp.int32(0)
        for i in range(docs):
            doc_row = jnp.where(start <= pos, start, doc_row)
            doc_first = jnp.where(start <= t0, start, doc_first)
            doc_last = jnp.where(start <= t0 + TILE - 1, start, doc_last)
            start = start + lengths[i]
        low = jnp.maximum(pos - (W - 1), doc_row) - (t0 - W)
        low2 = jnp.concatenate([low, low], axis=1)
        lane2 = jnp.concatenate([lane, lane], axis=1)

        def attend(count, packed):
            key_iota = lax.broadcasted_iota(jnp.int32, (TILE, 2 * TILE), 0)
            chunks = range(SPAN - count, SPAN)

            def scores_of(g):
                query = jnp.concatenate(
                    [
                        q_ref[:, 2 * g * HD : (2 * g + 1) * HD],
                        q_ref[:, (2 * g + 1) * HD : (2 * g + 2) * HD],
                    ],
                    axis=0,
                )
                scores = []
                for c in chunks:
                    key = kbuf[pl.ds(pl.multiple_of(off + c * TILE, TILE), TILE), g * HD : (g + 1) * HD]
                    s = lax.dot_general(
                        key, query, (((1,), (1,)), ((), ())), preferred_element_type=jnp.float32
                    )
                    if packed or c == 0:
                        s = jnp.where(key_iota >= low2 - c * TILE, s, MASKED)
                    if c == SPAN - 1:
                        s = jnp.where(key_iota <= lane2, s, MASKED)
                    scores.append(s)
                return scores

            def finish(g, scores):
                top = functools.reduce(
                    jnp.maximum, [jnp.max(s, axis=0, keepdims=True) for s in scores]
                )
                top2 = top * log2_scale
                total = jnp.zeros_like(top)
                mixed = jnp.zeros((HD, 2 * TILE), jnp.float32)
                for c, s in zip(chunks, scores):
                    p = jnp.exp2(s * log2_scale - top2)
                    total = total + jnp.sum(p, axis=0, keepdims=True)
                    value = vbuf[g * HD : (g + 1) * HD, pl.ds(pl.multiple_of(off + c * TILE, TILE), TILE)]
                    mixed = mixed + jnp.dot(
                        value, p.astype(jnp.bfloat16), preferred_element_type=jnp.float32
                    )
                mixed = mixed / total
                norm = top * score_scale + jnp.log(total)
                for half in range(2):
                    head = 2 * g + half
                    part = mixed[:, half * TILE : (half + 1) * TILE]
                    out_ref[:, head * HD : (head + 1) * HD] = part.T.astype(jnp.bfloat16)
                    norm_ref[head : head + 1, :] = norm[:, half * TILE : (half + 1) * TILE]

            every = [scores_of(g) for g in range(kv_heads)]
            for g in range(kv_heads):
                finish(g, every[g])

        skip = jnp.maximum(doc_first - (t0 - W), 0) // TILE
        plain = doc_last <= t0 - W + TILE

        @pl.when(plain)
        def _():
            attend(SPAN, False)

        few = skip >= SPAN - 3

        @pl.when(jnp.logical_not(plain) & few)
        def _():
            attend(3, True)

        @pl.when(jnp.logical_not(plain) & jnp.logical_not(few))
        def _():
            attend(SPAN, True)


def run_tiles(first, tiles, info, lengths, queries, keys, values, prefix_keys, prefix_values, carried):
    rows, query_width = queries.shape
    key_width = keys.shape[1]
    heads = query_width // HD
    per = BLK // TILE

    def moving(step, info, lengths):
        return (jnp.maximum(jnp.minimum(step + first, info[1] * per - 1), 0), 0)

    def out_map(step, info, lengths):
        return (step + first, 0)

    def norm_map(step, info, lengths):
        return (0, step + first)

    fixed = pl.BlockSpec((W, key_width), lambda step, info, lengths: (0, 0))
    in_specs = [
        pl.BlockSpec((TILE, query_width), moving),
        pl.BlockSpec((TILE, key_width), moving),
        pl.BlockSpec((TILE, key_width), moving),
        fixed,
        fixed,
    ]
    args = [queries, keys, values, prefix_keys, prefix_values]
    aliases = {}
    if carried:
        in_specs += [pl.BlockSpec(memory_space=pl.ANY)] * 2
        args += list(carried)
        aliases = {7: 0, 8: 1}
    length = W + tiles * TILE
    work = tiles * TILE * heads * (W + TILE)
    return pl.pallas_call(
        functools.partial(kernel, first, bool(carried)),
        out_shape=(
            jax.ShapeDtypeStruct((rows, query_width), jnp.bfloat16),
            jax.ShapeDtypeStruct((heads, rows), jnp.float32),
        ),
        grid_spec=pltpu.PrefetchScalarGridSpec(
            num_scalar_prefetch=2,
            grid=(tiles,),
            in_specs=in_specs,
            out_specs=[
                pl.BlockSpec((TILE, query_width), out_map),
                pl.BlockSpec((heads, TILE), norm_map),
            ],
            scratch_shapes=[
                pltpu.VMEM((length, key_width), jnp.bfloat16),
                pltpu.VMEM((key_width, length), jnp.bfloat16),
            ],
        ),
        input_output_aliases=aliases,
        compiler_params=pltpu.CompilerParams(
            dimension_semantics=("arbitrary",), vmem_limit_bytes=56 * 1024 * 1024
        ),
        cost_estimate=pl.CostEstimate(
            flops=4 * work * HD, transcendentals=work, bytes_accessed=4 * tiles * TILE * query_width
        ),
        name="window_attention",
    )(info, lengths, *args)


def local(queries, keys, values, doc_lengths, live_blocks):
    rows = queries.shape[0]
    shard = lax.axis_index("ctx")
    prev_keys, prev_values = from_behind((keys[rows - W :], values[rows - W :]), "ctx", 1)
    info = jnp.stack([shard * rows, live_blocks[shard]]).astype(jnp.int32)
    ahead = W // TILE
    carried = run_tiles(
        ahead, rows // TILE - ahead, info, doc_lengths, queries, keys, values, keys, values, None
    )
    return run_tiles(
        0, ahead, info, doc_lengths, queries, keys, values, prev_keys, prev_values, carried
    )


def solution(mesh):
    in_specs = (
        P(("groups", "ctx"), "head"),
        P(("groups", "ctx"), "head"),
        P(("groups", "ctx"), "head"),
        P("groups"),
        P("groups"),
    )
    out_specs = (P(("groups", "ctx"), "head"), P(("groups", "head"), "ctx"))
    return jax.shard_map(local, mesh=mesh, in_specs=in_specs, out_specs=out_specs, check_vma=False)
```
